32 devices in a mesh: seq: 8 (over z, x), wsh: 4 (over y, core).
Axes of the slice: x: 2, y: 2, z: 4, core: 2. Of those that a mesh axis runs over, the one named last changes fastest.
Arguments:
- hidden_in: bfloat16 [4, 1024, 1024], P('wsh', 'seq'), may hold values from -6 to 6
- cotangent: bfloat16 [4, 1024, 1024], P('wsh', 'seq'), may hold values from -6 to 6
- in_weight: bfloat16 [1024, 4384], P('wsh'), may hold values from -0.1875 to 0.1875
- out_weight: bfloat16 [2048, 1024], P('wsh'), may hold values from -0.125 to 0.125
- norm_gain: bfloat16 [1024], P('wsh'), may hold values from 0.5 to 1.5
- gate_gain: bfloat16 [2048], P('wsh'), may hold values from 0.5 to 1.5
- conv_weight: float32 [4, 2304], replicated, may hold values from -3 to 3
- conv_bias: float32 [2304], replicated, may hold values from -3 to 3
- dt_bias: float32 [32], replicated, may hold values from -6 to -1
- log_rate: float32 [32], replicated, may hold values from -4 to 1.5
- skip_gain: float32 [32], replicated, may hold values from 0.5 to 2
Outputs:
- block_out: bfloat16 [4, 1024, 1024], P('wsh', 'seq')
- d_hidden_in: bfloat16 [4, 1024, 1024], P('wsh', 'seq')
- g_in_weight: float32 [1024, 4384], P('wsh')
- g_out_weight: float32 [2048, 1024], P('wsh')
- g_norm_gain: float32 [1024], P('wsh')
- g_gate_gain: float32 [2048], P('wsh')
- g_conv_weight: float32 [4, 2304], replicated
- g_conv_bias: float32 [2304], replicated
- g_dt_bias: float32 [32], replicated
- g_log_rate: float32 [32], replicated
- g_skip_gain: float32 [32], replicated
The draws below stay inside these ranges and needn't reach their ends.
All inputs are finite; a program needn't handle non-finite values.
Results may differ from the reference program's by a relative error of at most 0.009.
Values may be sent and summed in bfloat16 or wider, within the bound.
No kernel may reach another device: no remote copies, remote signals or barrier semaphores. Data moves between devices by JAX's collectives and lax.ppermute only.
A program may use at most 192 MiB of HBM per device.

```python
import jax
import jax.numpy as jnp
from jax import lax

D = 1024
NH = 32
NSTATE = 128
KCONV = 4
SPAN = 128
DIN = 2048
PROJ = 4384
CONV = 2304
LENGTH = 1024
SEQS = 4


def levels(own_key, extent, split, smallest, largest):
    def one(position, parts):
        steps = jax.random.uniform(jax.random.fold_in(jax.random.fold_in(own_key, 6), position), (parts,), jnp.float32, smallest / len(split), largest / len(split))
        return jnp.repeat(jnp.exp(steps), extent[position] // parts).reshape((-1,) + (1,) * (len(extent) - position - 1))

    factor_of = one(*split[0])
    for cut in split[1:]:
        factor_of = factor_of * one(*cut)
    return factor_of


def gaussian(stream_key, extent, width, most, cuts=(), dtype=jnp.bfloat16):
    values = jax.random.normal(stream_key, extent, jnp.float32) * width
    if len(cuts) > 0:
        values = levels(stream_key, extent, cuts, -0.22, 0.18) * values
    return jnp.clip(values, min=-most, max=most).astype(dtype)


def setup_inputs(seed: int = 0) -> dict:
    key_list = jax.random.split(jax.random.key(seed), 12)
    hidden_in = gaussian(key_list[0], (SEQS, LENGTH, D), 1.0, 6.0, ((0, 4), (1, 8)))
    cotangent = gaussian(key_list[1], (SEQS, LENGTH, D), 1.0, 6.0, ((0, 4), (1, 8)))
    in_weight = gaussian(key_list[2], (D, PROJ), D ** -0.5, 0.1875, ((0, 4),))
    out_weight = gaussian(key_list[3], (DIN, D), DIN ** -0.5, 0.125, ((0, 4),))
    norm_gain = jnp.clip(1.0 + 0.1 * jax.random.normal(key_list[4], (D,), jnp.float32), 0.5, 1.5).astype(jnp.bfloat16)
    gate_gain = jnp.clip(1.0 + 0.1 * jax.random.normal(key_list[5], (DIN,), jnp.float32), 0.5, 1.5).astype(jnp.bfloat16)
    conv_weight = gaussian(key_list[6], (KCONV, CONV), 0.5, 3.0, (), jnp.float32)
    conv_bias = gaussian(key_list[7], (CONV,), 0.5, 3.0, (), jnp.float32)
    dt_bias = jnp.clip(jax.random.uniform(key_list[8], (NH,), jnp.float32, -6.0, -1.0), -6.0, -1.0)
    log_rate = jnp.clip(jax.random.uniform(key_list[9], (NH,), jnp.float32, -4.0, 1.5), -4.0, 1.5)
    skip_gain = jnp.clip(jax.random.uniform(key_list[10], (NH,), jnp.float32, 0.5, 2.0), 0.5, 2.0)
    return {"hidden_in": hidden_in, "cotangent": cotangent, "in_weight": in_weight, "out_weight": out_weight, "norm_gain": norm_gain, "gate_gain": gate_gain, "conv_weight": conv_weight, "conv_bias": conv_bias, "dt_bias": dt_bias, "log_rate": log_rate, "skip_gain": skip_gain}


EPSILON = 1e-05
PRECISE = lax.Precision.HIGHEST

def causal_conv(values, kernel, shift_bias):
    kernel_width = kernel.shape[0]
    length = values.shape[0]
    padded = jnp.pad(values, ((kernel_width - 1, 0), (0, 0)))
    running = jnp.zeros_like(values) + shift_bias[None, :]
    for offset in range(kernel_width):
        running = running + kernel[offset][None, :] * padded[offset:offset + length]
    return jax.nn.silu(running)

def state_scan(x_source, bc_source, dt_source, kernel_x, bias_x, kernel_bc, bias_bc, dt_shift, log_rates, skip_gains):
    length = x_source.shape[0]
    head_count = dt_source.shape[1]
    head_dim = x_source.shape[1] // head_count
    state_size = bc_source.shape[1] // 2
    x_conv = causal_conv(x_source, kernel_x, bias_x)
    bc_conv = causal_conv(bc_source, kernel_bc, bias_bc)
    steps_dt = jax.nn.softplus(dt_source + dt_shift[None, :])
    log_decay = -steps_dt * jnp.exp(log_rates)[None, :]
    blocks = length // SPAN
    x_scaled = x_conv.reshape(length, head_count, head_dim) * steps_dt[:, :, None]
    x_blocks = x_scaled.reshape(blocks, SPAN, head_count, head_dim)
    b_blocks = bc_conv[:, :state_size].reshape(blocks, SPAN, state_size)
    c_blocks = bc_conv[:, state_size:].reshape(blocks, SPAN, state_size)
    cumulative = jnp.cumsum(log_decay.reshape(blocks, SPAN, head_count), axis=1)
    cum_heads = jnp.swapaxes(cumulative, 1, 2)
    row_index = lax.broadcasted_iota(jnp.int32, (SPAN, SPAN), 0)
    col_index = lax.broadcasted_iota(jnp.int32, (SPAN, SPAN), 1)
    causal = (row_index >= col_index)[None, None, :, :]
    log_gap = cum_heads[:, :, :, None] - cum_heads[:, :, None, :]
    scores = jnp.einsum('ctn,csn->cts', c_blocks, b_blocks, precision=PRECISE)
    mixing = jnp.where(causal, jnp.exp(jnp.where(causal, log_gap, 0.0)), 0.0) * scores[:, None, :, :]
    inner_part = jnp.einsum('chts,cshp->cthp', mixing, x_blocks, precision=PRECISE)
    tail_weight = jnp.exp(cumulative[:, -1:, :] - cumulative)
    block_states = jnp.einsum('csn,csh,cshp->chnp', b_blocks, tail_weight, x_blocks, precision=PRECISE)
    carry_rate = jnp.exp(cumulative[:, -1, :])

    def advance(carried, element):
        block_rate, fresh_state = element
        return (block_rate[:, None, None] * carried + fresh_state, carried)
    start_state = jnp.zeros((head_count, state_size, head_dim), jnp.float32)
    _, entering = lax.scan(advance, start_state, (carry_rate, block_states))
    outer_part = jnp.einsum('ctn,chnp,cth->cthp', c_blocks, entering, jnp.exp(cumulative), precision=PRECISE)
    mixing_out = (inner_part + outer_part).reshape(length, head_count * head_dim)
    return mixing_out + x_conv * jnp.repeat(skip_gains, head_dim)[None, :]

def scan_single(packed):
    return state_scan(packed[0], packed[1], packed[2], packed[3], packed[4], packed[5], packed[6], packed[7], packed[8], packed[9])

def norm_in(token_rows, norm_scale):
    inv_rms = lax.rsqrt(lax.optimization_barrier(jnp.mean(token_rows * token_rows, axis=-1, keepdims=True)) + EPSILON)
    return token_rows * inv_rms * norm_scale[None, :]

def gated_norm(mixing_rows, gate_rows, norm_scale):
    gated_rows = mixing_rows * jax.nn.silu(gate_rows)
    inv_rms = lax.rsqrt(lax.optimization_barrier(jnp.mean(gated_rows * gated_rows, axis=-1, keepdims=True)) + EPSILON)
    return gated_rows * inv_rms * norm_scale[None, :]

def reference(hidden_in, cotangent, in_weight, out_weight, norm_gain, gate_gain, conv_weight, conv_bias, dt_bias, log_rate, skip_gain):
    gain_norm = norm_gain.astype(jnp.float32)
    gain_gated = gate_gain.astype(jnp.float32)

    def one_sequence(totals, inputs):
        hidden_seq, cot_seq = inputs
        hidden_f = hidden_seq.astype(jnp.float32)
        normed = norm_in(hidden_f, gain_norm).astype(jnp.bfloat16)
        projected = lax.optimization_barrier(jnp.dot(normed, in_weight, preferred_element_type=jnp.float32).astype(jnp.bfloat16))
        gate_part = projected[:, :DIN]
        x_part = projected[:, DIN:2 * DIN]
        bc_part = projected[:, 2 * DIN:2 * DIN + 2 * NSTATE]
        dt_part = projected[:, 2 * DIN + 2 * NSTATE:]
        packed = (x_part.astype(jnp.float32), bc_part.astype(jnp.float32), dt_part.astype(jnp.float32), conv_weight[:, :DIN], conv_bias[:DIN], conv_weight[:, DIN:], conv_bias[DIN:], dt_bias, log_rate, skip_gain)
        scanned, scan_back = jax.vjp(scan_single, packed)
        scanned_b = lax.optimization_barrier(scanned.astype(jnp.bfloat16))
        gated_out, gate_back = jax.vjp(gated_norm, scanned_b.astype(jnp.float32), gate_part.astype(jnp.float32), gain_gated)
        gated_b = gated_out.astype(jnp.bfloat16)
        branch_out = jnp.dot(gated_b, out_weight, preferred_element_type=jnp.float32)
        block_seq = (hidden_f + branch_out).astype(jnp.bfloat16)
        d_gated = jnp.dot(cot_seq, out_weight.T, preferred_element_type=jnp.float32)
        g_out = jnp.dot(gated_b.T, cot_seq, preferred_element_type=jnp.float32)
        d_scanned, d_gate, g_gate = gate_back(d_gated)
        grads = scan_back(d_scanned)[0]
        d_projected = jnp.concatenate([d_gate, grads[0], grads[1], grads[2]], axis=1).astype(jnp.bfloat16)
        d_normed = jnp.dot(d_projected, in_weight.T, preferred_element_type=jnp.float32)
        g_in = jnp.dot(normed.T, d_projected, preferred_element_type=jnp.float32)
        _, norm_back = jax.vjp(norm_in, hidden_f, gain_norm)
        d_norm_in, g_norm = norm_back(d_normed)
        d_hidden_seq = (cot_seq.astype(jnp.float32) + d_norm_in).astype(jnp.bfloat16)
        conv_grad = jnp.concatenate([grads[3], grads[5]], axis=1)
        conv_bias_grad = jnp.concatenate([grads[4], grads[6]], axis=0)
        updates = (g_in, g_out, g_norm, g_gate, conv_grad, conv_bias_grad, grads[7], grads[8], grads[9])
        totals = tuple((total_part + update_part for total_part, update_part in zip(totals, updates)))
        return (totals, (block_seq, d_hidden_seq))
    zeros_init = (jnp.zeros((D, PROJ), jnp.float32), jnp.zeros((DIN, D), jnp.float32), jnp.zeros((D,), jnp.float32), jnp.zeros((DIN,), jnp.float32), jnp.zeros((KCONV, CONV), jnp.float32), jnp.zeros((CONV,), jnp.float32), jnp.zeros((NH,), jnp.float32), jnp.zeros((NH,), jnp.float32), jnp.zeros((NH,), jnp.float32))
    totals, (block_out, d_hidden_in) = lax.scan(one_sequence, zeros_init, (hidden_in, cotangent))
    return (block_out, d_hidden_in, totals[0], totals[1], totals[2], totals[3], totals[4], totals[5], totals[6], totals[7], totals[8])
```

```python
import functools

import jax
import jax.numpy as jnp
from jax import lax
from jax.experimental import pallas as pl
from jax.experimental.pallas import tpu as pltpu
from jax.sharding import PartitionSpec as P

NH = 32
NSTATE = 128
KCONV = 4
SPAN = 128
DIN = 2048
PROJ = 4384
HALO = 16
EPSILON = 1e-05


f32 = jnp.float32
b16 = jnp.bfloat16
NN = (((1,), (0,)), ((), ()))
NT = (((1,), (1,)), ((), ()))
TN = (((0,), (0,)), ((), ()))


def mm(a, b, dims):
    return lax.dot_general(a.astype(b16), b.astype(b16), dims, preferred_element_type=f32)


def mm_left_split(a, b, dims):
    high = a.astype(b16)
    low = (a - high.astype(f32)).astype(b16)
    return mm(high, b, dims) + mm(low, b, dims)


def mm_right_split(a, b, dims):
    high = b.astype(b16)
    low = (b - high.astype(f32)).astype(b16)
    return mm(a, high, dims) + mm(a, low, dims)


def mm_right_exact(a, b, dims):
    high = b.astype(b16)
    rest = b - high.astype(f32)
    mid = rest.astype(b16)
    low = (rest - mid.astype(f32)).astype(b16)
    return mm(a, high, dims) + mm(a, mid, dims) + mm(a, low, dims)


def sigmoid(x):
    return 1.0 / (1.0 + jnp.exp(-x))


def softplus(x):
    return jnp.maximum(x, 0.0) + jnp.log1p(jnp.exp(-jnp.abs(x)))


def conv_window(proj_ref, ubuf, c, first, last):
    start = pl.multiple_of(c * SPAN, SPAN)
    prior = pl.multiple_of(jnp.maximum(start - HALO, 0), HALO)
    keep = jnp.where(c > 0, 1.0, 0.0)
    ubuf[0:HALO, :] = proj_ref[pl.ds(prior, HALO), first:last].astype(f32) * keep
    ubuf[HALO:, :] = proj_ref[pl.ds(start, SPAN), first:last].astype(f32)


def conv_pre(ubuf, cw_ref, cb_ref):
    pre = cb_ref[...]
    for k in range(KCONV):
        off = HALO - KCONV + 1 + k
        pre = pre + cw_ref[k : k + 1, :] * ubuf[off : off + SPAN, :]
    return pre


def steps(proj_ref, rows, width, sel_ref, dtb_ref, rate_ref):
    raw = mm(proj_ref[rows, 2 * width + 2 * NSTATE :], sel_ref[...], NN) + dtb_ref[...]
    sd = softplus(raw)
    return raw, sd, -sd * rate_ref[...]


def triangles():
    r = lax.broadcasted_iota(jnp.int32, (SPAN, SPAN), 0)
    c = lax.broadcasted_iota(jnp.int32, (SPAN, SPAN), 1)
    return r >= c, r > c, r <= c


def decay_matrix(lower, cum, cum_t, lane):
    gap = cum[:, lane : lane + 1] - cum_t[lane : lane + 1, :]
    return jnp.exp(jnp.where(lower, gap, -1e30))


def forward_kernel(heads, proj_ref, cw_ref, cb_ref, sel_ref, dtb_ref, rate_ref, skip_ref,
                   sc_ref, ent_ref, state, ubuf):
    width = skip_ref.shape[1]
    hd = width // heads
    blocks = proj_ref.shape[0] // SPAN
    state[...] = jnp.zeros_like(state)
    lower, _, _ = triangles()
    ones_low = jnp.where(lower, 1.0, 0.0).astype(b16)

    def step(c, carry):
        rows = pl.ds(pl.multiple_of(c * SPAN, SPAN), SPAN)
        conv_window(proj_ref, ubuf, c, width, 2 * width + 2 * NSTATE)
        pre = conv_pre(ubuf, cw_ref, cb_ref)
        uc = pre * sigmoid(pre)
        xc = uc[:, :width]
        bm = uc[:, width : width + NSTATE].astype(b16)
        cm = uc[:, width + NSTATE :].astype(b16)
        _, sd, ld = steps(proj_ref, rows, width, sel_ref, dtb_ref, rate_ref)
        cum = mm_right_exact(ones_low, ld, NN)
        cum_t = jnp.transpose(cum)
        tot = cum[SPAN - 1 : SPAN, :]
        xs = xc * sd
        xs_b = xs.astype(b16)
        scores = mm(cm, bm, NT)
        enter = state[...]
        inner = []
        for h in range(heads):
            mix = decay_matrix(lower, cum, cum_t, h * hd) * scores
            inner.append(mm(mix, xs_b[:, h * hd : (h + 1) * hd], NN))
        y = jnp.concatenate(inner, axis=1) + mm(cm, enter, NN) * jnp.exp(cum)
        sc_ref[rows, :] = (y + skip_ref[...] * xc).astype(b16)
        ent_ref[pl.ds(c, 1)] = enter[None]
        state[...] = jnp.exp(tot) * enter + mm(bm, xs * jnp.exp(tot - cum), TN)
        return carry

    lax.fori_loop(0, blocks, step, 0)


def backward_kernel(heads, proj_ref, dy_ref, ent_ref, cw_ref, cb_ref, sel_ref, selt_ref, dtb_ref,
                    rate_ref, skip_ref, dproj_ref, gconv_ref, ghead_ref, dstate, ubuf, dbuf, gbuf):
    width = skip_ref.shape[1]
    hd = width // heads
    blocks = proj_ref.shape[0] // SPAN
    dstate[...] = jnp.zeros_like(dstate)
    dbuf[...] = jnp.zeros_like(dbuf)
    gconv_ref[...] = jnp.zeros_like(gconv_ref)
    ghead_ref[...] = jnp.zeros_like(ghead_ref)
    lower, strict, upper = triangles()
    ones_low = jnp.where(lower, 1.0, 0.0).astype(b16)
    ones_up = jnp.where(upper, 1.0, 0.0).astype(b16)
    strict_f = jnp.where(strict, 1.0, 0.0)
    strict_all = jnp.concatenate([strict_f] * heads, axis=1)
    gr = lax.broadcasted_iota(jnp.int32, (heads * SPAN, width), 0) // SPAN
    gc = lax.broadcasted_iota(jnp.int32, (heads * SPAN, width), 1) // hd
    spread = jnp.where(gr == gc, 1.0, 0.0).astype(b16)
    hr = lax.broadcasted_iota(jnp.int32, (width, width), 0) // hd
    hc = lax.broadcasted_iota(jnp.int32, (width, width), 1) // hd
    same = jnp.where(hr == hc, 1.0, 0.0).astype(b16)
    last_row = lax.broadcasted_iota(jnp.int32, (SPAN, width), 0) == SPAN - 1

    def step(i, carry):
        c = blocks - 1 - i
        rows = pl.ds(pl.multiple_of(c * SPAN, SPAN), SPAN)
        conv_window(proj_ref, ubuf, c, width, 2 * width + 2 * NSTATE)
        pre = conv_pre(ubuf, cw_ref, cb_ref)
        sig = sigmoid(pre)
        uc = pre * sig
        dsil = sig * (1.0 + pre * (1.0 - sig))
        xc = uc[:, :width]
        bm = uc[:, width : width + NSTATE].astype(b16)
        cm = uc[:, width + NSTATE :].astype(b16)
        raw, sd, ld = steps(proj_ref, rows, width, sel_ref, dtb_ref, rate_ref)
        cum = mm_right_exact(ones_low, ld, NN)
        cum_t = jnp.transpose(cum)
        tot = cum[SPAN - 1 : SPAN, :]
        ecum = jnp.exp(cum)
        etot = jnp.exp(tot)
        wgt = jnp.exp(tot - cum)
        xs = xc * sd
        xs_b = xs.astype(b16)
        dy = dy_ref[rows, :]
        dy_b = dy.astype(b16)
        enter = ent_ref[pl.ds(c, 1)][0]
        enter_b = enter.astype(b16)
        dst = dstate[...]
        dst_b = dst.astype(b16)
        scores = mm(cm, bm, NT)
        dscores = jnp.zeros((SPAN, SPAN), f32)
        dinner = []
        for h in range(heads):
            cols = slice(h * hd, (h + 1) * hd)
            dec = decay_matrix(lower, cum, cum_t, h * hd)
            mix = dec * scores
            dmd = mm(dy_b[:, cols], xs_b[:, cols], NT) * dec
            dscores = dscores + dmd
            gbuf[:, h * SPAN : (h + 1) * SPAN] = (dmd * scores * strict_f).astype(b16)
            dinner.append(mm(mix, dy_b[:, cols], TN))
        crossing = mm(ones_up, gbuf[...], NN) * strict_all
        dl = mm(crossing, spread, NN)
        bd = mm(bm, dst_b, NN) * wgt
        dxs = jnp.concatenate(dinner, axis=1) + bd
        dz = dy * ecum
        dz_b = dz.astype(b16)
        dscores_b = dscores.astype(b16)
        dcm = mm(dscores_b, bm, NN) + mm(dz_b, enter_b, NT)
        dbm = mm(dscores_b, cm, TN) + mm(xs * wgt, dst_b, NT)
        xbd = xs * bd
        dtot = etot * jnp.sum(dst * enter, axis=0, keepdims=True) + jnp.sum(xbd, axis=0, keepdims=True)
        v = dz * mm(cm, enter_b, NN) - xbd + jnp.where(last_row, dtot, 0.0)
        dl = dl + mm_left_split(mm_right_split(ones_up, v, NN), same, NN)
        dstate[...] = etot * dst + mm(cm, dz_b, TN)
        dxc = dxs * sd + skip_ref[...] * dy
        dsd = mm_left_split(dxs * xc, same, NN) - dl * rate_ref[...]
        draw = dsd * sigmoid(raw)
        ghead_ref[0:1, :] += jnp.sum(draw, axis=0, keepdims=True)
        ghead_ref[1:2, :] += jnp.sum(dl * ld, axis=0, keepdims=True)
        ghead_ref[2:3, :] += jnp.sum(dy * xc, axis=0, keepdims=True)
        du = jnp.concatenate([dxc, dbm, dcm], axis=1) * dsil
        dbuf[0:SPAN, :] = du
        dx = jnp.zeros_like(du)
        for k in range(KCONV):
            off = KCONV - 1 - k
            dx = dx + cw_ref[k : k + 1, :] * dbuf[off : off + SPAN, :]
            back = HALO - KCONV + 1 + k
            gconv_ref[k : k + 1, :] += jnp.sum(du * ubuf[back : back + SPAN, :], axis=0, keepdims=True)
        gconv_ref[KCONV : KCONV + 1, :] += jnp.sum(du, axis=0, keepdims=True)
        dbuf[SPAN : SPAN + 8, :] = du[0:8, :]
        dproj_ref[rows, : width + 2 * NSTATE] = dx.astype(b16)
        dproj_ref[rows, width + 2 * NSTATE :] = mm(draw, selt_ref[...], NN).astype(b16)
        return carry

    lax.fori_loop(0, blocks, step, 0)


VM = pl.BlockSpec(memory_space=pltpu.VMEM)


def scan_forward(proj, cw, cb, sel, dtb, rate, skip, heads):
    length = proj.shape[0]
    width = skip.shape[1]
    mixed = width + 2 * NSTATE
    blocks = length // SPAN
    return pl.pallas_call(
        functools.partial(forward_kernel, heads),
        name="scan_fwd",
        out_shape=(
            jax.ShapeDtypeStruct((length, width), b16),
            jax.ShapeDtypeStruct((blocks, NSTATE, width), f32),
        ),
        in_specs=[VM] * 7,
        out_specs=(VM, VM),
        scratch_shapes=[pltpu.VMEM((NSTATE, width), f32), pltpu.VMEM((HALO + SPAN, mixed), f32)],
    )(proj, cw, cb, sel, dtb, rate, skip)


def scan_backward(proj, dy, ent, cw, cb, sel, selt, dtb, rate, skip, heads):
    length = proj.shape[0]
    width = skip.shape[1]
    mixed = width + 2 * NSTATE
    return pl.pallas_call(
        functools.partial(backward_kernel, heads),
        name="scan_bwd",
        out_shape=(
            jax.ShapeDtypeStruct((length, mixed + NH), b16),
            jax.ShapeDtypeStruct((8, mixed), f32),
            jax.ShapeDtypeStruct((8, width), f32),
        ),
        in_specs=[VM] * 10,
        out_specs=(VM, VM, VM),
        scratch_shapes=[
            pltpu.VMEM((NSTATE, width), f32),
            pltpu.VMEM((HALO + SPAN, mixed), f32),
            pltpu.VMEM((SPAN + 8, mixed), f32),
            pltpu.VMEM((SPAN, heads * SPAN), b16),
        ],
    )(proj, dy, ent, cw, cb, sel, selt, dtb, rate, skip)


def place(pieces, slots):
    rows = pieces[0].shape[0]
    whole = jnp.zeros((rows * len(pieces),) + pieces[0].shape[1:], pieces[0].dtype)
    for piece, slot in zip(pieces, slots):
        whole = lax.dynamic_update_slice_in_dim(whole, piece, slot * rows, 0)
    return whole


def gather_rows(x, axis):
    n = lax.axis_size(axis)
    me = lax.axis_index(axis)
    pairs = n // 2
    major = me // 2
    swap = [(i, i ^ 1) for i in range(n)]
    pieces = [x]
    slots = [me]
    order = []
    for k in range(1, pairs):
        order.append(k // 2 + 1 if k % 2 else pairs - k // 2)
    for k in order:
        turn = [(i, ((i // 2 + k) % pairs) * 2 + i % 2) for i in range(n)]
        pieces.append(lax.ppermute(x, axis, turn))
        slots.append(((major - k + pairs) % pairs) * 2 + me % 2)
    for j in range(pairs):
        pieces.append(lax.ppermute(pieces[j], axis, swap))
        slots.append(slots[j] ^ 1)
    return place(pieces, slots)


def gather_rows_pair(x, axis):
    n = lax.axis_size(axis)
    me = lax.axis_index(axis)
    pairs = n // 2
    major = me // 2
    swap = [(i, i ^ 1) for i in range(n)]
    pieces = [x]
    slots = [me]
    for k in range(1, pairs):
        turn = [(i, ((i // 2 + k) % pairs) * 2 + i % 2) for i in range(n)]
        pieces.append(lax.ppermute(x, axis, turn))
        slots.append(((major - k + pairs) % pairs) * 2 + me % 2)
    rows = x.shape[0]
    both = lax.ppermute(jnp.concatenate(pieces, axis=0), axis, swap)
    other = [both[j * rows : (j + 1) * rows] for j in range(pairs)]
    return place(pieces + other, slots + [s ^ 1 for s in slots])


def swap_blocks(x, axis):
    return lax.all_to_all(x, axis, split_axis=0, concat_axis=0, tiled=True)


def scatter_sum(blocks, axis):
    return jnp.sum(swap_blocks(blocks, axis).astype(f32), axis=0)


def shards(hidden_in, cotangent, in_weight, out_weight, norm_gain, gate_gain, conv_weight,
           conv_bias, dt_bias, log_rate, skip_gain):
    ns = lax.axis_size("seq")
    nw = lax.axis_size("wsh")
    si = lax.axis_index("seq")
    seqs, tok, width = hidden_in.shape
    assert seqs == 1
    length = tok * ns
    gw = DIN // ns
    hg = NH // ns
    hd = DIN // NH
    in_rows = width // nw
    out_rows = DIN // nw
    ratio = out_rows // in_rows
    shared = 2 * NSTATE + NH
    start = si * gw
    hidden = hidden_in[0]
    cot = cotangent[0]

    mine = jnp.concatenate(
        [
            lax.dynamic_slice_in_dim(in_weight, start, gw, 1),
            lax.dynamic_slice_in_dim(in_weight, DIN + start, gw, 1),
            in_weight[:, 2 * DIN :],
            norm_gain[:, None],
            gate_gain.reshape(in_rows, ratio),
        ],
        axis=1,
    )
    hidden_all = gather_rows(hidden, "seq")
    mine_all = gather_rows_pair(mine, "wsh")
    w_mine = mine_all[:, : 2 * gw + shared]
    gain_norm = mine_all[:, 2 * gw + shared].astype(f32)
    gain_gate = mine_all[:, 2 * gw + shared + 1 :].reshape(DIN)
    gain_mine = lax.dynamic_slice_in_dim(gain_gate, start, gw, 0).astype(f32)[None, :]
    out_all = gather_rows_pair(out_weight, "wsh")
    in_all = gather_rows_pair(in_weight, "wsh")
    cot_all = gather_rows(cot, "seq")

    rep = lambda a: jnp.repeat(lax.dynamic_slice_in_dim(a, si * hg, hg, 0), hd)[None, :]
    cw = jnp.concatenate([lax.dynamic_slice_in_dim(conv_weight, start, gw, 1), conv_weight[:, DIN:]], axis=1)
    cb = jnp.concatenate([lax.dynamic_slice_in_dim(conv_bias, start, gw, 0), conv_bias[DIN:]])[None, :]
    dtb, rate, skip = rep(dt_bias), jnp.exp(rep(log_rate)), rep(skip_gain)
    head_of = si * hg + lax.broadcasted_iota(jnp.int32, (NH, gw), 1) // hd
    sel = (lax.broadcasted_iota(jnp.int32, (NH, gw), 0) == head_of).astype(b16)
    first = (lax.broadcasted_iota(jnp.int32, (gw, NH), 0) % hd) == 0
    head_t = si * hg + lax.broadcasted_iota(jnp.int32, (gw, NH), 0) // hd
    selt = (first & (head_t == lax.broadcasted_iota(jnp.int32, (gw, NH), 1))).astype(b16)

    hid_f = hidden_all.astype(f32)
    inv = lax.rsqrt(jnp.mean(hid_f * hid_f, axis=-1, keepdims=True) + EPSILON)
    normed = (hid_f * inv * gain_norm[None, :]).astype(b16)
    proj = jnp.dot(normed, w_mine, preferred_element_type=f32).astype(b16)
    scanned, entering = scan_forward(proj, cw, cb, sel, dtb, rate, skip, hg)
    gate = proj[:, :gw].astype(f32)
    gate_sig = jax.nn.sigmoid(gate)
    gate_silu = gate * gate_sig
    sc = scanned.astype(f32)
    q = sc * gate_silu
    out_mine = lax.dynamic_slice_in_dim(out_all, start, gw, 0)
    dy = jnp.einsum("td,id->ti", cot_all, out_mine, preferred_element_type=f32) * gain_mine
    part = jnp.stack([jnp.sum(q * q, axis=1), jnp.sum(dy * q, axis=1)])
    stats = jnp.sum(swap_blocks(jnp.broadcast_to(part[None], (ns,) + part.shape), "seq"), axis=0)
    r = lax.rsqrt(stats[0] * (1.0 / DIN) + EPSILON)[:, None]
    k2 = stats[1][:, None] * (r * r * r) * (1.0 / DIN)
    gated = (q * r * gain_mine).astype(b16)
    dq = r * dy - q * k2
    d_scan = dq * gate_silu
    d_gate = (dq * sc * (gate_sig * (1.0 + gate * (1.0 - gate_sig)))).astype(b16)

    to_tok = jnp.concatenate([gated, d_gate], axis=1).reshape(ns, tok, 2 * gw)
    from_heads = swap_blocks(to_tok, "seq")
    gated_tok = jnp.swapaxes(from_heads[:, :, :gw], 0, 1).reshape(tok, DIN)
    d_gate_tok = jnp.swapaxes(from_heads[:, :, gw:], 0, 1).reshape(tok, DIN)
    branch = jnp.dot(gated_tok, out_all, preferred_element_type=f32)
    block_out = (hidden.astype(f32) + branch).astype(b16)[None]
    gi_gate = jnp.einsum("td,te->de", normed, d_gate, preferred_element_type=f32).astype(b16)
    go = jnp.einsum("ti,td->id", gated, cot_all, preferred_element_type=f32).astype(b16)
    gi_gate_rows = scatter_sum(gi_gate.reshape(nw, in_rows, gw), "wsh").astype(b16)
    go_cols = scatter_sum(
        jnp.swapaxes(go.reshape(gw, nw, width // nw), 0, 1), "wsh"
    ).astype(b16)
    early = gather_rows(jnp.concatenate([gi_gate_rows.reshape(-1, 128), go_cols.reshape(-1, 128)]), "seq")
    early = early.reshape(ns, -1)
    gi_gate_all = early[:, : in_rows * gw].reshape(ns, in_rows, gw)
    go_all = early[:, in_rows * gw :].reshape(nw, out_rows, width // nw)
    go_mine = swap_blocks(go_all, "wsh")
    g_out = jnp.swapaxes(go_mine, 0, 1).reshape(out_rows, width).astype(f32)

    d_rest, g_conv, g_head = scan_backward(
        proj, d_scan, entering, cw, cb, sel, selt, dtb, rate, skip, hg
    )
    rest = d_rest.shape[1]
    tok_parts = swap_blocks(d_rest.reshape(ns, tok, rest), "seq")
    d_x_tok = jnp.swapaxes(tok_parts[:, :, :gw], 0, 1).reshape(tok, DIN)
    d_shared_tok = jnp.sum(tok_parts[:, :, gw:].astype(f32), axis=0).astype(b16)
    d_proj = jnp.concatenate([d_gate_tok, d_x_tok, d_shared_tok], axis=1)
    d_normed = jnp.einsum("te,de->td", d_proj, in_all, preferred_element_type=f32)
    hid_l = hidden.astype(f32)
    inv_l = lax.rsqrt(jnp.mean(hid_l * hid_l, axis=-1, keepdims=True) + EPSILON)
    dng = d_normed * gain_norm[None, :]
    d_norm_in = inv_l * dng - hid_l * (inv_l * inv_l * inv_l) * jnp.mean(dng * hid_l, axis=-1, keepdims=True)
    d_hidden = (cot.astype(f32) + d_norm_in).astype(b16)[None]

    gi_rest = jnp.einsum("td,te->de", normed, d_rest, preferred_element_type=f32).astype(b16)
    gi_rest_rows = scatter_sum(gi_rest.reshape(nw, in_rows, rest), "wsh")
    small = jnp.concatenate([g_conv[: KCONV + 1].reshape(-1), g_head[:3].reshape(-1)])
    small = jnp.pad(small, (0, -small.shape[0] % 1024)).reshape(-1, 128)
    small_w = jnp.sum(swap_blocks(jnp.broadcast_to(small[None], (nw,) + small.shape), "wsh"), axis=0)
    small_hi = small_w.astype(b16)
    small_lo = (small_w - small_hi.astype(f32)).astype(b16)
    late = jnp.concatenate([gi_rest_rows.astype(b16).reshape(-1, 128), small_hi, small_lo])
    late = gather_rows(late, "seq").reshape(ns, -1)
    gi_late = late[:, : in_rows * rest].reshape(ns, in_rows, rest)
    sm = small_hi.size
    tail = late[:, in_rows * rest :].astype(f32)
    small_all = tail[:, :sm] + tail[:, sm : 2 * sm]
    g_in = jnp.concatenate(
        [
            jnp.swapaxes(gi_gate_all, 0, 1).reshape(in_rows, DIN).astype(f32),
            jnp.swapaxes(gi_late[:, :, :gw], 0, 1).reshape(in_rows, DIN).astype(f32),
            jnp.sum(gi_late[:, :, gw:].astype(f32), axis=0),
        ],
        axis=1,
    )
    g_norm = jnp.sum(in_weight.astype(f32) * g_in, axis=1) / norm_gain.astype(f32)
    g_gate = jnp.sum(out_weight.astype(f32) * g_out, axis=1) / gate_gain.astype(f32)

    mixed = gw + 2 * NSTATE
    conv_all = small_all[:, : (KCONV + 1) * mixed].reshape(ns, KCONV + 1, mixed)
    conv_full = jnp.concatenate(
        [
            jnp.swapaxes(conv_all[:, :, :gw], 0, 1).reshape(KCONV + 1, DIN),
            jnp.sum(conv_all[:, :, gw:], axis=0),
        ],
        axis=1,
    )
    heads_all = small_all[:, (KCONV + 1) * mixed : (KCONV + 1) * mixed + 3 * gw].reshape(ns, 3, hg, hd)
    g_dtb = heads_all[:, 0, :, 0].reshape(NH)
    g_rate = heads_all[:, 1, :, 0].reshape(NH)
    g_skip = jnp.sum(heads_all[:, 2], axis=-1).reshape(NH)
    return (
        block_out,
        d_hidden,
        g_in,
        g_out,
        g_norm,
        g_gate,
        conv_full[:KCONV],
        conv_full[KCONV],
        g_dtb,
        g_rate,
        g_skip,
    )


def solution(mesh):
    tokens = P("wsh", "seq", None)
    specs = (tokens, tokens, P("wsh", None), P("wsh", None), P("wsh"), P("wsh"))
    return jax.shard_map(
        shards, mesh=mesh, in_specs=specs + (P(),) * 5, out_specs=specs + (P(),) * 5, check_vma=False
    )
```
